128 devices in a mesh: ctx: 16 (over z, y), head: 8 (over x, core).
Axes of the slice: x: 4, y: 4, z: 4, core: 2. Of those that a mesh axis runs over, the one named last changes fastest.
Arguments:
- query_states: bfloat16 [16384, 128, 128], P(('ctx', 'head')), may hold values from -8 to 8
- key_states: bfloat16 [16384, 8, 128], P(('ctx', 'head')), may hold values from -8 to 8
- value_states: bfloat16 [16384, 8, 128], P(('ctx', 'head')), may hold values from -6 to 6
- slash_offsets: int32 [8, 256, 12], P('head'), may hold values from 0 to 31, as said below
- slash_counts: int32 [8, 256], P('head'), may hold values from 1 to 12, as said below
- vertical_blocks: int32 [8, 256, 12], P('head'), may hold values from 0 to 223, as said below
- vertical_counts: int32 [8, 256], P('head'), may hold values from 0 to 12, as said below
Outputs:
- attended: bfloat16 [16384, 128, 128], P(('ctx', 'head'))
The draws below stay inside these ranges and needn't reach their ends.
Inputs may be any that keep to these rules, and one draw needn't show every extreme that they name: `slash_offsets`: for every head and query block b, the entries j < slash_counts are distinct, at most b and below 32; entry 0 is 0; the other entries are 0. `slash_counts`: at most min(12, b + 1) for query block b. `vertical_blocks`: for every head and query block b, the entries j < vertical_counts are distinct blocks at most b - 32; the other entries are 0. `vertical_counts`: at most max(0, b - 31) for query block b.
All inputs are finite; a program needn't handle non-finite values.
Results may differ from the reference program's by a relative error of at most 0.0049.
Values may be sent and summed in bfloat16 or wider, within the bound.
A program may use at most 128 MiB of HBM per device.

```python
import jax
import jax.numpy as jnp
from jax import lax

HQ = 128
KVH = 8
HD = 128
BLK = 64
NS = 12
NV = 12
SEQ = 16384
QBLK = 256
SPAN = 32
G = 16


def pattern(key):
    base = jax.random.fold_in(key, 11)
    rows = jnp.arange(QBLK, dtype=jnp.int32)[None, :, None]
    row_ids = jnp.arange(QBLK, dtype=jnp.int32)[None, :]
    slash_cand = jnp.arange(SPAN, dtype=jnp.int32)[None, None, :]
    slash_noise = jax.random.randint(jax.random.fold_in(base, 1), (KVH, QBLK, SPAN), 0, 65536)
    slash_score = slash_noise * SPAN + (SPAN - 1 - slash_cand)
    slash_score = jnp.where(slash_cand == SPAN - 1, 2 ** 30 - 1, slash_score)
    slash_score = jnp.where(slash_cand == 0, 2 ** 30, slash_score)
    slash_score = jnp.where(slash_cand <= rows, slash_score, -1 - slash_cand)
    slash_pick = lax.top_k(slash_score, NS)[1].astype(jnp.int32)
    slash_extra = jax.random.randint(jax.random.fold_in(base, 2), (KVH, QBLK), 0, 4)
    slash_count = jnp.minimum(jnp.minimum(row_ids + 1, NS), 1 + row_ids * NS // QBLK + slash_extra).astype(jnp.int32)
    slash_slot = jnp.arange(NS, dtype=jnp.int32)[None, None, :]
    slash_list = jnp.where(slash_slot < slash_count[:, :, None], slash_pick, 0).astype(jnp.int32)
    vert_cand = jnp.arange(QBLK, dtype=jnp.int32)[None, None, :]
    vert_noise = jax.random.randint(jax.random.fold_in(base, 3), (KVH, QBLK, QBLK), 0, 65536)
    vert_score = vert_noise * QBLK + (QBLK - 1 - vert_cand)
    vert_score = jnp.where(vert_cand == rows - SPAN, 2 ** 30, vert_score)
    vert_score = jnp.where(vert_cand <= rows - SPAN, vert_score, -1 - vert_cand)
    vert_pick = lax.top_k(vert_score, NV)[1].astype(jnp.int32)
    vert_extra = jax.random.randint(jax.random.fold_in(base, 4), (KVH, QBLK), 0, 4)
    vert_count = jnp.minimum(jnp.minimum(jnp.maximum(row_ids - SPAN + 1, 0), NV), 1 + row_ids * NV // QBLK + vert_extra).astype(jnp.int32)
    vert_slot = jnp.arange(NV, dtype=jnp.int32)[None, None, :]
    vert_list = jnp.where(vert_slot < vert_count[:, :, None], vert_pick, 0).astype(jnp.int32)
    return (slash_list, slash_count, vert_list, vert_count)


def draw_slash_offsets(key, part):
    return pattern(key)[0]


def draw_slash_counts(key, part):
    return pattern(key)[1]


def draw_vertical_blocks(key, part):
    return pattern(key)[2]


def draw_vertical_counts(key, part):
    return pattern(key)[3]


def draw_query_states(key, part):
    shape = (SEQ, HQ, HD)
    return jnp.clip(jax.random.normal(jax.random.fold_in(key, 1), shape, jnp.float32), -4.5, 4.5).astype(jnp.bfloat16)


def draw_key_states(key, part):
    shape = (SEQ, KVH, HD)
    return jnp.clip(jax.random.normal(jax.random.fold_in(key, 6), shape, jnp.float32), -4.5, 4.5).astype(jnp.bfloat16)


def shard_levels(own_key, dims, pieces, low, largest):
    def one(dim, blocks):
        draws = jax.random.uniform(jax.random.fold_in(jax.random.fold_in(own_key, 6), dim), (blocks,), jnp.float32, low / len(pieces), largest / len(pieces))
        return jnp.repeat(jnp.exp(draws), dims[dim] // blocks).reshape((-1,) + (1,) * (len(dims) - dim - 1))

    loudness = one(*pieces[0])
    for cut in pieces[1:]:
        loudness = loudness * one(*cut)
    return loudness


def normal_values(own_key, dims, deviation, reach, cuts=(), kind=jnp.bfloat16):
    level = shard_levels(own_key, dims, cuts, -0.22, 0.18) if cuts else 1.0
    values = jax.random.normal(own_key, dims, jnp.float32) * deviation * level
    return jnp.minimum(jnp.maximum(values, -reach), reach).astype(kind)


def setup_inputs(seed: int = 0) -> dict:
    keys = jax.random.split(jax.random.key(seed), 8)
    return {
        "query_states": draw_query_states(jax.random.fold_in(keys[7], 71), 0),
        "key_states": draw_key_states(jax.random.fold_in(keys[7], 71), 0),
        "value_states": normal_values(keys[2], (SEQ, KVH, HD), 1.0, 6.0, ((0, 128),)),
        "slash_offsets": draw_slash_offsets(jax.random.fold_in(keys[7], 71), 0),
        "slash_counts": draw_slash_counts(jax.random.fold_in(keys[7], 71), 0),
        "vertical_blocks": draw_vertical_blocks(jax.random.fold_in(keys[7], 71), 0),
        "vertical_counts": draw_vertical_counts(jax.random.fold_in(keys[7], 71), 0),
    }


NEG = -1.0e30


def reference(query_states, key_states, value_states, slash_offsets, slash_counts, vertical_blocks, vertical_counts):
    head_dim = query_states.shape[2]
    kv_heads = key_states.shape[1]
    query_grid = query_states.reshape(QBLK, BLK, kv_heads, G, head_dim)
    key_grid = key_states.reshape(QBLK, BLK, kv_heads, head_dim)
    value_grid = value_states.reshape(QBLK, BLK, kv_heads, head_dim)
    factor = head_dim ** -0.5
    within = jnp.arange(BLK, dtype=jnp.int32)

    def one_block(head_index, block_index):
        chosen = jnp.concatenate([block_index - slash_offsets[head_index, block_index], vertical_blocks[head_index, block_index]]).astype(jnp.int32)
        live_slots = jnp.concatenate([jnp.arange(NS, dtype=jnp.int32) < slash_counts[head_index, block_index], jnp.arange(NV, dtype=jnp.int32) < vertical_counts[head_index, block_index]])
        key_tiles = key_grid[chosen, :, head_index].astype(jnp.float32).reshape(-1, head_dim)
        value_tiles = value_grid[chosen, :, head_index].astype(jnp.float32).reshape(-1, head_dim)
        query_tile = query_grid[block_index, :, head_index].astype(jnp.float32)
        scores = jnp.einsum('qgd,sd->gqs', query_tile, key_tiles) * factor
        key_pos = (chosen[:, None] * BLK + within[None, :]).reshape(-1)
        key_live = jnp.repeat(live_slots, BLK)
        query_pos = block_index * BLK + within
        visible = key_live[None, :] & (key_pos[None, :] <= query_pos[:, None])
        masked = jnp.where(visible[None], scores, NEG)
        row_max = jnp.max(masked, axis=-1, keepdims=True)
        probs = jnp.where(visible[None], jnp.exp(scores - row_max), 0.0)
        totals = jnp.sum(probs, axis=-1)
        rounded = lax.optimization_barrier(probs.astype(jnp.bfloat16)).astype(jnp.float32)
        summed = jnp.einsum('gqs,sd->qgd', rounded, value_tiles)
        return (summed / jnp.transpose(totals)[:, :, None]).astype(jnp.bfloat16)

    heads_flat = jnp.repeat(jnp.arange(kv_heads, dtype=jnp.int32), QBLK).reshape(-1, 8)
    blocks_flat = jnp.tile(jnp.arange(QBLK, dtype=jnp.int32), kv_heads).reshape(-1, 8)
    result = lax.map(lambda entries: jax.vmap(one_block)(entries[0], entries[1]), (heads_flat, blocks_flat))
    result = result.reshape(kv_heads, QBLK, BLK, G, head_dim)
    return jnp.transpose(result, (1, 2, 0, 3, 4)).reshape(QBLK * BLK, kv_heads * G, head_dim)
```

```python
import functools
import math

import jax
import jax.numpy as jnp
from jax import lax
from jax.experimental import pallas as pl
from jax.experimental.pallas import tpu as pltpu
from jax.sharding import PartitionSpec as P

BLK = 64
G = 16
NS = 12
NV = 12
HD = 128
SLOTS = NS + NV
KEYS = SLOTS * BLK
ROWS = 512
NEG = -1e30
FACTOR = HD ** -0.5 * math.log2(math.e)


def attention_kernel(
    so_ref, sc_ref, vb_ref, vc_ref, q_ref, k_ref, v_ref, o_ref, kg, vg, scores, tops
):
    blocks = q_ref.shape[0]
    first = lax.axis_index("ctx") * blocks

    def fetch(i, side):
        b = first + i
        slash_live = sc_ref[0, b]
        vertical_live = vc_ref[0, b]
        for j in range(SLOTS):
            if j < NS:
                block = b - so_ref[0, b, j]
                live = j < slash_live
            else:
                block = vb_ref[0, b, j - NS]
                live = j - NS < vertical_live
            here = pl.ds(j * BLK, BLK)
            kg[side, here, :HD] = k_ref[block]
            bias = jnp.where(live, 0.0, NEG).astype(jnp.float32)
            kg[side, here, HD:] = jnp.full((BLK, HD), bias, jnp.float32).astype(jnp.bfloat16)
            vg[side, here, :HD] = v_ref[block]

    def score(i, half, side):
        tokens = ROWS // G
        queries = q_ref[i, pl.ds(half * tokens, tokens)].reshape(ROWS, HD)
        pick = (lax.broadcasted_iota(jnp.int32, (ROWS, HD), 1) == 0).astype(jnp.bfloat16)
        lhs = jnp.concatenate([queries, pick], axis=1)
        got = lax.dot_general(
            lhs, kg[side], (((1,), (1,)), ((), ())), preferred_element_type=jnp.float32
        )
        row = lax.broadcasted_iota(jnp.int32, (ROWS, 2 * BLK), 0) // G + half * tokens
        col = lax.broadcasted_iota(jnp.int32, (ROWS, 2 * BLK), 1)
        edge = jnp.where((col >= BLK) | (col <= row), got[:, : 2 * BLK], NEG)
        scores[half, :, : 2 * BLK] = edge
        scores[half, :, 2 * BLK :] = got[:, 2 * BLK :]
        top = jnp.maximum(
            jnp.max(edge, axis=1, keepdims=True), jnp.max(got[:, 2 * BLK :], axis=1, keepdims=True)
        )
        tops[half] = jnp.broadcast_to(top * FACTOR, (ROWS, HD))

    def answer(i, half, side):
        tokens = ROWS // G
        top = jnp.concatenate([tops[half]] * (KEYS // HD), axis=1)
        probs = jnp.exp2(scores[half] * FACTOR - top).astype(jnp.bfloat16)
        got = jnp.dot(probs, vg[side], preferred_element_type=jnp.float32)
        out = (got[:, :HD] / got[:, HD:]).astype(jnp.bfloat16)
        o_ref[i, pl.ds(half * tokens, tokens)] = out.reshape(tokens, G, HD)

    vg[:, :, HD:] = jnp.ones((2, KEYS, HD), jnp.bfloat16)
    fetch(0, 0)
    score(0, 0, 0)

    def step(i, carry):
        side = lax.rem(i, 2)
        score(i, 1, side)
        answer(i, 0, side)
        later = jnp.minimum(i + 1, blocks - 1)
        fetch(later, 1 - side)
        score(later, 0, 1 - side)
        answer(i, 1, side)
        return carry

    lax.fori_loop(0, blocks, step, 0)


def attention(query, keys, values, so, sc, vb, vc):
    smem = pl.BlockSpec(memory_space=pltpu.SMEM)
    vmem = pl.BlockSpec(memory_space=pltpu.VMEM)
    return pl.pallas_call(
        attention_kernel,
        out_shape=jax.ShapeDtypeStruct(query.shape, query.dtype),
        in_specs=[smem] * 4 + [vmem] * 3,
        out_specs=vmem,
        scratch_shapes=[
            pltpu.VMEM((2, KEYS, 2 * HD), jnp.bfloat16),
            pltpu.VMEM((2, KEYS, 2 * HD), jnp.bfloat16),
            pltpu.VMEM((2, ROWS, KEYS), jnp.float32),
            pltpu.VMEM((2, ROWS, HD), jnp.float32),
        ],
        compiler_params=pltpu.CompilerParams(vmem_limit_bytes=60 << 20),
    )(so, sc, vb, vc, query, keys, values)


def on_device(query_states, key_states, value_states, so, sc, vb, vc):
    def exchange(x):
        return lax.all_to_all(x, "head", split_axis=1, concat_axis=0, tiled=True)

    key_local, value_local = exchange(key_states), exchange(value_states)
    key_full = lax.all_gather(key_local, "ctx", axis=0, tiled=True)
    value_full = lax.all_gather(value_local, "ctx", axis=0, tiled=True)
    query_local = exchange(query_states)
    rows = query_local.shape[0]
    answers = attention(
        query_local.reshape(rows // BLK, BLK, G, HD),
        key_full.reshape(-1, BLK, HD),
        value_full.reshape(-1, BLK, HD),
        so, sc, vb, vc,
    )
    return lax.all_to_all(
        answers.reshape(rows, G, HD), "head", split_axis=0, concat_axis=1, tiled=True
    )


def solution(mesh):
    token = P(("ctx", "head"), None, None)
    in_specs = (token,) * 3 + (P("head", None, None), P("head", None)) * 2
    return jax.shard_map(
        on_device, mesh=mesh, in_specs=in_specs, out_specs=token, check_vma=False
    )
```

```python
import math

import jax
import jax.numpy as jnp
from jax import lax
from jax.experimental import pallas as pl
from jax.experimental.pallas import tpu as pltpu
from jax.sharding import PartitionSpec as P

BLK = 64
G = 16
NS = 12
NV = 12
HD = 128
SLOTS = NS + NV
KEYS = SLOTS * BLK
ROWS = 512
RING = 4
HEADS = 2 * RING
SHARD = 2 * HEADS
BLOCKS = RING * RING * SHARD
NEG = -1e30
FACTOR = HD ** -0.5 * math.log2(math.e)
MESH = pl.DeviceIdType.MESH
PARTNERS = ((2, 0), (2, 1), (1, 0), (3, 0), (1, 1), (3, 1), (0, 1), (0, 0))


def remote(src, dst, send, recv, device):
    return pltpu.make_async_remote_copy(
        src_ref=src, dst_ref=dst, send_sem=send, recv_sem=recv, device_id=device, device_id_type=MESH
    )


def kernel(
    so_ref, sc_ref, vb_ref, vc_ref, q_ref, kv_ref, o_ref,
    qs, kv, os, kg, vg, scores, tops,
    q_send, q_recv, kv_send, kv_recv, o_send, o_recv,
):
    me, head = lax.axis_index("ctx"), lax.axis_index("head")
    z, y = lax.div(me, RING), lax.rem(me, RING)
    x, core = lax.div(head, 2), lax.rem(head, 2)

    def place(dz, dy):
        return lax.rem(z + dz + RING, RING) * RING + lax.rem(y + dy + RING, RING)

    def partner(dx, other):
        return lax.rem(x + dx, RING) * 2 + lax.rem(core + other, 2)

    peers = [(me, partner(dx, other)) for dx, other in PARTNERS[:-1]]
    peers += [(place(0, 1), head), (place(0, -1), head), (place(1, 0), head), (place(-1, 0), head)]
    barrier = pltpu.get_barrier_semaphore()
    for peer in peers:
        pl.semaphore_signal(barrier, inc=1, device_id=peer, device_id_type=MESH)
    pl.semaphore_wait(barrier, len(peers))

    mine = pl.ds(me * SHARD + head * 2, 2)
    sent = []
    entry = []
    for n, (dx, other) in enumerate(PARTNERS[:-1]):
        to = partner(dx, other)
        copy = remote(kv_ref.at[to], kv.at[:, mine], kv_send.at[n], kv_recv.at[n], (me, to))
        copy.start()
        entry.append(copy)
    queries = []
    for n, (dx, other) in enumerate(PARTNERS[:-1]):
        to = partner(dx, other)
        copy = remote(
            q_ref.at[:, pl.ds(pl.multiple_of(to * G, G), G)], qs.at[head],
            q_send.at[n], q_recv.at[n], (me, to),
        )
        copy.start()
        queries.append(copy)
    own_q = pltpu.make_async_copy(
        q_ref.at[:, pl.ds(pl.multiple_of(head * G, G), G)], qs.at[head], q_send.at[7]
    )
    own_q.start()
    own_kv = pltpu.make_async_copy(kv_ref.at[head], kv.at[:, mine], kv_send.at[7])
    own_kv.start()
    own_kv.wait()
    for copy in entry:
        copy.wait_recv()
    sent += entry

    count = len(PARTNERS)

    def pass_on(which, shard, low, length, device):
        nonlocal count
        piece = kv.at[which, pl.ds(shard * SHARD + low, length)]
        copy = remote(piece, piece, kv_send.at[count], kv_recv.at[count], device)
        count += 1
        copy.start()
        sent.append(copy)
        return copy

    def at(which, first, second):
        return place(second, first) if which == 0 else place(first, second)

    half = SHARD // 2
    first = {}
    second = {}
    for which in (0, 1):
        for d in (1, -1):
            first[which, d] = pass_on(which, me, 0, SHARD, (at(which, d, 0), head))
    for which in (0, 1):
        for d in (1, -1):
            second[which, 0, d] = pass_on(which, me, 0, SHARD, (at(which, 0, d), head))
    first_far = []
    for d in (1, -1):
        for which in (0, 1):
            first[which, d].wait_recv()
            shard = at(which, -d, 0)
            low = 0 if d == 1 else half
            first_far.append(pass_on(which, shard, low, half, (at(which, d, 0), head)))
            for e in (1, -1):
                second[which, -d, e] = pass_on(which, shard, 0, SHARD, (at(which, 0, e), head))
    second_far = []

    def relay(line):
        for which in (0, 1):
            for e in (1, -1):
                second[which, line, e].wait_recv()
                low = 0 if e == 1 else half
                second_far.append(
                    pass_on(which, at(which, line, -e), low, half, (at(which, 0, e), head))
                )

    relay(0)
    for copy in first_far:
        copy.wait_recv()
    for which in (0, 1):
        for e in (1, -1):
            second[which, 2, e] = pass_on(which, at(which, 2, 0), 0, SHARD, (at(which, 0, e), head))
    for line in (-1, 1, 2):
        relay(line)
    for copy in second_far:
        copy.wait_recv()
    for copy in queries:
        copy.wait_recv()
    own_q.wait()

    def turn(i):
        n = lax.div(i, 2)
        dx = jnp.where(n < 2, 2, jnp.where(n < 6, 1 + 2 * lax.rem(n, 2), 0))
        other = jnp.where((n == 1) | ((n >= 4) & (n <= 6)), 1, 0)
        return partner(dx, other), lax.rem(i, 2)

    def fetch(i, side):
        source, part = turn(i)
        b = me * SHARD + source * 2 + part
        slash_live = sc_ref[0, b]
        vertical_live = vc_ref[0, b]
        for j in range(SLOTS):
            if j < NS:
                block = b - so_ref[0, b, j]
                live = j < slash_live
            else:
                block = vb_ref[0, b, j - NS]
                live = j - NS < vertical_live
            here = pl.ds(j * BLK, BLK)
            kg[side, here, :HD] = kv[0, block]
            bias = jnp.where(live, 0.0, NEG).astype(jnp.float32)
            kg[side, here, HD:] = jnp.full((BLK, HD), bias, jnp.float32).astype(jnp.bfloat16)
            vg[side, here, :HD] = kv[1, block]

    tokens = ROWS // G

    def score(i, half, side):
        source, part = turn(i)
        rows = qs[source, pl.ds(part * BLK + half * tokens, tokens)].reshape(ROWS, HD)
        pick = (lax.broadcasted_iota(jnp.int32, (ROWS, HD), 1) == 0).astype(jnp.bfloat16)
        lhs = jnp.concatenate([rows, pick], axis=1)
        got = lax.dot_general(
            lhs, kg[side], (((1,), (1,)), ((), ())), preferred_element_type=jnp.float32
        )
        row = lax.broadcasted_iota(jnp.int32, (ROWS, 2 * BLK), 0) // G + half * tokens
        col = lax.broadcasted_iota(jnp.int32, (ROWS, 2 * BLK), 1)
        edge = jnp.where((col >= BLK) | (col <= row), got[:, : 2 * BLK], NEG)
        scores[half, :, : 2 * BLK] = edge
        scores[half, :, 2 * BLK :] = got[:, 2 * BLK :]
        top = jnp.maximum(
            jnp.max(edge, axis=1, keepdims=True), jnp.max(got[:, 2 * BLK :], axis=1, keepdims=True)
        )
        tops[half] = jnp.broadcast_to(top * FACTOR, (ROWS, HD))

    def answer(i, half, side):
        source, part = turn(i)
        top = jnp.concatenate([tops[half]] * (KEYS // HD), axis=1)
        probs = jnp.exp2(scores[half] * FACTOR - top).astype(jnp.bfloat16)
        got = jnp.dot(probs, vg[side], preferred_element_type=jnp.float32)
        out = (got[:, :HD] / got[:, HD:]).astype(jnp.bfloat16)
        os[source, pl.ds(part * BLK + half * tokens, tokens)] = out.reshape(tokens, G, HD)

    columns = pl.ds(pl.multiple_of(head * G, G), G)

    def give(i):
        source, part = turn(i)
        rows = pl.ds(part * BLK, BLK)
        return remote(
            os.at[source, rows], o_ref.at[rows, columns], o_send.at[i], o_recv.at[i], (me, source)
        )

    def keep(part):
        rows = pl.ds(part * BLK, BLK)
        return pltpu.make_async_copy(
            os.at[head, rows], o_ref.at[rows, columns], o_send.at[SHARD - 2 + part]
        )

    vg[:, :, HD:] = jnp.ones((2, KEYS, HD), jnp.bfloat16)
    fetch(0, 0)
    score(0, 0, 0)

    def step(i, carry):
        side = lax.rem(i, 2)
        score(i, 1, side)

        @pl.when((i >= 1) & (i <= SHARD - 2))
        def _():
            give(i - 1).start()

        answer(i, 0, side)
        later = jnp.minimum(i + 1, SHARD - 1)
        fetch(later, 1 - side)
        score(later, 0, 1 - side)
        answer(i, 1, side)
        return carry

    lax.fori_loop(0, SHARD, step, 0)
    for part in range(2):
        keep(part).start()
    for copy in sent + queries:
        copy.wait_send()
    for part in range(2):
        keep(part).wait()

    def finish(i, carry):
        give(i).wait()
        return carry

    lax.fori_loop(0, SHARD - 2, finish, 0)


def on_device(query_states, key_states, value_states, so, sc, vb, vc):
    rows = query_states.shape[0]

    def by_head(a):
        return jnp.transpose(a, (1, 0, 2)).reshape(HEADS, 1, rows // BLK, BLK, HD)

    kv = jnp.concatenate([by_head(key_states), by_head(value_states)], axis=1)
    smem = pl.BlockSpec(memory_space=pltpu.SMEM)
    hbm = pl.BlockSpec(memory_space=pl.ANY)
    bf16 = jnp.bfloat16
    return pl.pallas_call(
        kernel,
        out_shape=jax.ShapeDtypeStruct(query_states.shape, query_states.dtype),
        in_specs=[smem] * 4 + [hbm] * 2,
        out_specs=hbm,
        scratch_shapes=[
            pltpu.VMEM((HEADS, 2 * BLK, G, HD), bf16),
            pltpu.VMEM((2, BLOCKS, BLK, HD), bf16),
            pltpu.VMEM((HEADS, 2 * BLK, G, HD), bf16),
            pltpu.VMEM((2, KEYS, 2 * HD), bf16),
            pltpu.VMEM((2, KEYS, 2 * HD), bf16),
            pltpu.VMEM((2, ROWS, KEYS), jnp.float32),
            pltpu.VMEM((2, ROWS, HD), jnp.float32),
            pltpu.SemaphoreType.DMA((8,)),
            pltpu.SemaphoreType.DMA((8,)),
            pltpu.SemaphoreType.DMA((48,)),
            pltpu.SemaphoreType.DMA((48,)),
            pltpu.SemaphoreType.DMA((SHARD,)),
            pltpu.SemaphoreType.DMA((SHARD,)),
        ],
        compiler_params=pltpu.CompilerParams(
            collective_id=0, has_side_effects=True, vmem_limit_bytes=60 << 20
        ),
    )(so, sc, vb, vc, query_states, kv)


def solution(mesh):
    token = P(("ctx", "head"), None, None)
    in_specs = (token,) * 3 + (P("head", None, None), P("head", None)) * 2
    return jax.shard_map(
        on_device, mesh=mesh, in_specs=in_specs, out_specs=token, check_vma=False
    )
```

```python
import math

import jax
import jax.numpy as jnp
from jax import lax
from jax.experimental import pallas as pl
from jax.experimental.pallas import tpu as pltpu
from jax.sharding import PartitionSpec as P

BLK = 64
G = 16
NS = 12
NV = 12
HD = 128
SLOTS = NS + NV
KEYS = SLOTS * BLK
ROWS = 512
RING = 4
HEADS = 2 * RING
SHARD = 2 * HEADS
BLOCKS = RING * RING * SHARD
NEG = -1e30
FACTOR = HD ** -0.5 * math.log2(math.e)
MESH = pl.DeviceIdType.MESH
PARTNERS = ((2, 0), (2, 1), (1, 0), (3, 0), (1, 1), (3, 1), (0, 1), (0, 0))


def remote(src, dst, send, recv, device):
    return pltpu.make_async_remote_copy(
        src_ref=src, dst_ref=dst, send_sem=send, recv_sem=recv, device_id=device, device_id_type=MESH
    )


def kernel(
    so_hbm, sc_hbm, vb_hbm, vc_hbm, q_ref, k_hbm, v_hbm, o_ref,
    so_ref, sc_ref, vb_ref, vc_ref, k_ref, v_ref, kv_ref, qs, kv, os, kg, vg, scores, tops,
    q_send, q_recv, kv_send, kv_recv, o_send, o_recv, local,
):
    me, head = lax.axis_index("ctx"), lax.axis_index("head")
    z, y = lax.div(me, RING), lax.rem(me, RING)
    x, core = lax.div(head, 2), lax.rem(head, 2)

    tables = [
        pltpu.make_async_copy(src, dst, local.at[n])
        for n, (src, dst) in enumerate(
            ((k_hbm, k_ref), (v_hbm, v_ref), (so_hbm, so_ref), (sc_hbm, sc_ref), (vb_hbm, vb_ref), (vc_hbm, vc_ref))
        )
    ]
    for copy in tables:
        copy.start()

    def place(dz, dy):
        return lax.rem(z + dz + RING, RING) * RING + lax.rem(y + dy + RING, RING)

    def partner(dx, other):
        return lax.rem(x + dx, RING) * 2 + lax.rem(core + other, 2)

    peers = [(me, partner(dx, other)) for dx, other in PARTNERS[:-1]]
    peers += [(place(0, 1), head), (place(0, -1), head), (place(1, 0), head), (place(-1, 0), head)]
    barrier = pltpu.get_barrier_semaphore()
    for peer in peers:
        pl.semaphore_signal(barrier, inc=1, device_id=peer, device_id_type=MESH)
    for copy in tables[:2]:
        copy.wait()
    for which, ref in ((0, k_ref), (1, v_ref)):
        for n in range(HEADS):
            kv_ref[n, which] = ref[:, n, :].reshape(2, BLK, HD)
    pl.semaphore_wait(barrier, len(peers))

    mine = pl.ds(me * SHARD + head * 2, 2)
    sent = []
    entry = []
    for n, (dx, other) in enumerate(PARTNERS[:-1]):
        to = partner(dx, other)
        copy = remote(kv_ref.at[to], kv.at[:, mine], kv_send.at[n], kv_recv.at[n], (me, to))
        copy.start()
        entry.append(copy)
    queries = []
    for n, (dx, other) in enumerate(PARTNERS[:-1]):
        to = partner(dx, other)
        copy = remote(
            q_ref.at[:, pl.ds(pl.multiple_of(to * G, G), G)], qs.at[head],
            q_send.at[n], q_recv.at[n], (me, to),
        )
        copy.start()
        queries.append(copy)
    own_q = pltpu.make_async_copy(
        q_ref.at[:, pl.ds(pl.multiple_of(head * G, G), G)], qs.at[head], q_send.at[7]
    )
    own_q.start()
    own_kv = pltpu.make_async_copy(kv_ref.at[head], kv.at[:, mine], kv_send.at[7])
    own_kv.start()
    own_kv.wait()
    for copy in entry:
        copy.wait_recv()
    sent += entry

    count = len(PARTNERS)

    def pass_on(which, shard, low, length, device):
        nonlocal count
        piece = kv.at[which, pl.ds(shard * SHARD + low, length)]
        copy = remote(piece, piece, kv_send.at[count], kv_recv.at[count], device)
        count += 1
        copy.start()
        sent.append(copy)
        return copy

    def at(which, first, second):
        return place(second, first) if which == 0 else place(first, second)

    half = SHARD // 2
    first = {}
    second = {}
    for which in (0, 1):
        for d in (1, -1):
            first[which, d] = pass_on(which, me, 0, SHARD, (at(which, d, 0), head))
    for which in (0, 1):
        for d in (1, -1):
            second[which, 0, d] = pass_on(which, me, 0, SHARD, (at(which, 0, d), head))
    first_far = []
    for d in (1, -1):
        for which in (0, 1):
            first[which, d].wait_recv()
            shard = at(which, -d, 0)
            low = 0 if d == 1 else half
            first_far.append(pass_on(which, shard, low, half, (at(which, d, 0), head)))
            for e in (1, -1):
                second[which, -d, e] = pass_on(which, shard, 0, SHARD, (at(which, 0, e), head))
    second_far = []

    def relay(line):
        for which in (0, 1):
            for e in (1, -1):
                second[which, line, e].wait_recv()
                low = 0 if e == 1 else half
                second_far.append(
                    pass_on(which, at(which, line, -e), low, half, (at(which, 0, e), head))
                )

    relay(0)
    for copy in first_far:
        copy.wait_recv()
    for which in (0, 1):
        for e in (1, -1):
            second[which, 2, e] = pass_on(which, at(which, 2, 0), 0, SHARD, (at(which, 0, e), head))
    for line in (-1, 1, 2):
        relay(line)
    for copy in second_far:
        copy.wait_recv()
    for copy in queries:
        copy.wait_recv()
    own_q.wait()
    for copy in tables[2:]:
        copy.wait()

    def turn(i):
        n = lax.div(i, 2)
        dx = jnp.where(n < 2, 2, jnp.where(n < 6, 1 + 2 * lax.rem(n, 2), 0))
        other = jnp.where((n == 1) | ((n >= 4) & (n <= 6)), 1, 0)
        return partner(dx, other), lax.rem(i, 2)

    def fetch(i, side):
        source, part = turn(i)
        b = me * SHARD + source * 2 + part
        slash_live = sc_ref[0, b]
        vertical_live = vc_ref[0, b]
        for j in range(SLOTS):
            if j < NS:
                block = b - so_ref[j, 0, b]
                live = j < slash_live
            else:
                block = vb_ref[j - NS, 0, b]
                live = j - NS < vertical_live
            here = pl.ds(j * BLK, BLK)
            kg[side, here, :HD] = kv[0, block]
            bias = jnp.where(live, 0.0, NEG).astype(jnp.float32)
            kg[side, here, HD:] = jnp.full((BLK, HD), bias, jnp.float32).astype(jnp.bfloat16)
            vg[side, here, :HD] = kv[1, block]

    tokens = ROWS // G

    def score(i, half, side):
        source, part = turn(i)
        rows = qs[source, pl.ds(part * BLK + half * tokens, tokens)].reshape(ROWS, HD)
        pick = (lax.broadcasted_iota(jnp.int32, (ROWS, HD), 1) == 0).astype(jnp.bfloat16)
        lhs = jnp.concatenate([rows, pick], axis=1)
        got = lax.dot_general(
            lhs, kg[side], (((1,), (1,)), ((), ())), preferred_element_type=jnp.float32
        )
        row = lax.broadcasted_iota(jnp.int32, (ROWS, 2 * BLK), 0) // G + half * tokens
        col = lax.broadcasted_iota(jnp.int32, (ROWS, 2 * BLK), 1)
        edge = jnp.where((col >= BLK) | (col <= row), got[:, : 2 * BLK], NEG)
        scores[half, :, : 2 * BLK] = edge
        scores[half, :, 2 * BLK :] = got[:, 2 * BLK :]
        top = jnp.maximum(
            jnp.max(edge, axis=1, keepdims=True), jnp.max(got[:, 2 * BLK :], axis=1, keepdims=True)
        )
        tops[half] = jnp.broadcast_to(top * FACTOR, (ROWS, HD))

    def answer(i, half, side):
        source, part = turn(i)
        top = jnp.concatenate([tops[half]] * (KEYS // HD), axis=1)
        probs = jnp.exp2(scores[half] * FACTOR - top).astype(jnp.bfloat16)
        got = jnp.dot(probs, vg[side], preferred_element_type=jnp.float32)
        out = (got[:, :HD] / got[:, HD:]).astype(jnp.bfloat16)
        os[source, pl.ds(part * BLK + half * tokens, tokens)] = out.reshape(tokens, G, HD)

    columns = pl.ds(pl.multiple_of(head * G, G), G)

    def give(i):
        source, part = turn(i)
        rows = pl.ds(part * BLK, BLK)
        return remote(
            os.at[source, rows], o_ref.at[rows, columns], o_send.at[i], o_recv.at[i], (me, source)
        )

    def keep(part):
        rows = pl.ds(part * BLK, BLK)
        return pltpu.make_async_copy(
            os.at[head, rows], o_ref.at[rows, columns], o_send.at[SHARD - 2 + part]
        )

    vg[:, :, HD:] = jnp.ones((2, KEYS, HD), jnp.bfloat16)
    fetch(0, 0)
    score(0, 0, 0)

    def step(i, carry):
        side = lax.rem(i, 2)
        score(i, 1, side)

        @pl.when((i >= 1) & (i <= SHARD - 2))
        def _():
            give(i - 1).start()

        answer(i, 0, side)
        later = jnp.minimum(i + 1, SHARD - 1)
        fetch(later, 1 - side)
        score(later, 0, 1 - side)
        answer(i, 1, side)
        return carry

    lax.fori_loop(0, SHARD, step, 0)
    for part in range(2):
        keep(part).start()
    for copy in sent + queries:
        copy.wait_send()
    for part in range(2):
        keep(part).wait()

    def finish(i, carry):
        give(i).wait()
        return carry

    lax.fori_loop(0, SHARD - 2, finish, 0)


def on_device(query_states, key_states, value_states, so, sc, vb, vc):
    hbm = pl.BlockSpec(memory_space=pl.ANY)
    vmem = pl.BlockSpec(memory_space=pltpu.VMEM)
    bf16 = jnp.bfloat16
    so, vb = jnp.transpose(so, (2, 0, 1)), jnp.transpose(vb, (2, 0, 1))
    return pl.pallas_call(
        kernel,
        out_shape=pltpu.VMEM(query_states.shape, query_states.dtype),
        in_specs=[hbm] * 7,
        out_specs=vmem,
        scratch_shapes=[
            pltpu.SMEM(so.shape, jnp.int32),
            pltpu.SMEM(sc.shape, jnp.int32),
            pltpu.SMEM(vb.shape, jnp.int32),
            pltpu.SMEM(vc.shape, jnp.int32),
            pltpu.VMEM(key_states.shape, bf16),
            pltpu.VMEM(value_states.shape, bf16),
            pltpu.VMEM((HEADS, 2, 2, BLK, HD), bf16),
            pltpu.VMEM((HEADS, 2 * BLK, G, HD), bf16),
            pltpu.VMEM((2, BLOCKS, BLK, HD), bf16),
            pltpu.VMEM((HEADS, 2 * BLK, G, HD), bf16),
            pltpu.VMEM((2, KEYS, 2 * HD), bf16),
            pltpu.VMEM((2, KEYS, 2 * HD), bf16),
            pltpu.VMEM((2, ROWS, KEYS), jnp.float32),
            pltpu.VMEM((2, ROWS, HD), jnp.float32),
            pltpu.SemaphoreType.DMA((8,)),
            pltpu.SemaphoreType.DMA((8,)),
            pltpu.SemaphoreType.DMA((48,)),
            pltpu.SemaphoreType.DMA((48,)),
            pltpu.SemaphoreType.DMA((SHARD,)),
            pltpu.SemaphoreType.DMA((SHARD,)),
            pltpu.SemaphoreType.DMA((6,)),
        ],
        compiler_params=pltpu.CompilerParams(
            collective_id=0, has_side_effects=True, vmem_limit_bytes=62_700_000
        ),
    )(so, sc, vb, vc, query_states, key_states, value_states)


def solution(mesh):
    token = P(("ctx", "head"), None, None)
    in_specs = (token,) * 3 + (P("head", None, None), P("head", None)) * 2
    return jax.shard_map(
        on_device, mesh=mesh, in_specs=in_specs, out_specs=token, check_vma=False
    )
```

```python
import math

import jax
import jax.numpy as jnp
from jax import lax
from jax.experimental import pallas as pl
from jax.experimental.pallas import tpu as pltpu
from jax.sharding import PartitionSpec as P

BLK = 64
G = 16
NS = 12
NV = 12
HD = 128
SLOTS = NS + NV
KEYS = SLOTS * BLK
ROWS = 512
RING = 4
HEADS = 2 * RING
SHARD = 2 * HEADS
BLOCKS = RING * RING * SHARD
NEG = -1e30
FACTOR = HD ** -0.5 * math.log2(math.e)
MESH = pl.DeviceIdType.MESH
PARTNERS = ((2, 0), (2, 1), (1, 0), (3, 0), (1, 1), (3, 1), (0, 1), (0, 0))

STREAMS = ((0, 0, 16, True), (1, 0, 8, True), (1, 8, 8, False))
BATCHES = (2, 2, 2, 2, 2, 2)


def remote(src, dst, send, recv, device):
    return pltpu.make_async_remote_copy(
        src_ref=src, dst_ref=dst, send_sem=send, recv_sem=recv, device_id=device, device_id_type=MESH
    )


def kernel(
    so_hbm, sc_hbm, vb_hbm, vc_hbm, q_ref, k_hbm, v_hbm, o_ref,
    so_ref, sc_ref, vb_ref, vc_ref, so_in, sc_in, vb_in, vc_in, k_ref, v_ref, kv_ref, qs, kv, os, kg, vg, scores, tops,
    q_send, q_recv, kv_send, kv_recv, o_send, o_recv, local, t_send, t_recv,
):
    me, head = lax.axis_index("ctx"), lax.axis_index("head")
    z, y = lax.div(me, RING), lax.rem(me, RING)
    x, core = lax.div(head, 2), lax.rem(head, 2)

    def wrap(a):
        return lax.rem(a + RING, RING)

    def place(dz, dy):
        return wrap(z + dz) * RING + wrap(y + dy)

    def seat(dx, other):
        return wrap(x + dx) * 2 + lax.rem(core + other, 2)

    def served(d, other):
        return lax.rem(x + y + d + RING, RING) * 2 + lax.rem(core + other, 2)

    def partner(axis, d, other):
        return (me, seat(d, other)) if axis == 0 else (place(0, d), seat(0, other))

    def slant(d):
        return place(0, d), seat(-d, 0)

    loads = [
        pltpu.make_async_copy(src, dst, local.at[n])
        for n, (src, dst) in enumerate(((k_hbm, k_ref), (v_hbm, v_ref)))
    ]
    for copy in loads:
        copy.start()

    peers = [partner(0, d, other) for d, other in PARTNERS[:-1]]
    peers += [partner(1, d, other) for d, other in PARTNERS[:-2]]
    peers += [slant(1), slant(-1), (place(1, 0), head), (place(-1, 0), head)]
    barrier = pltpu.get_barrier_semaphore()
    for peer in peers:
        pl.semaphore_signal(barrier, inc=1, device_id=peer, device_id_type=MESH)
    for copy in loads:
        copy.wait()
    for which, ref in ((0, k_ref), (1, v_ref)):
        for n in range(HEADS):
            kv_ref[n, which] = ref[:, n, :].reshape(2, BLK, HD)
    pl.semaphore_wait(barrier, len(peers))

    mine = pl.ds(me * SHARD + head * 2, 2)
    sent = []
    entry = []
    for n, (d, other) in enumerate(PARTNERS[:-1]):
        copy = remote(
            kv_ref.at[served(d, other)], kv.at[:, mine], kv_send.at[n], kv_recv.at[n], partner(0, d, other)
        )
        copy.start()
        entry.append(copy)
    own_kv = pltpu.make_async_copy(kv_ref.at[served(0, 0)], kv.at[:, mine], kv_send.at[7])
    own_kv.start()
    tables = ((so_hbm, so_in, so_ref), (sc_hbm, sc_in, sc_ref), (vb_hbm, vb_in, vb_ref), (vc_hbm, vc_in, vc_ref))

    def here(n):
        return pltpu.make_async_copy(tables[n][0], tables[n][1], t_send.at[n])

    def there(n):
        return remote(tables[n][0], tables[n][1], t_send.at[4 + n], t_recv.at[n], (me, seat(-y, 0)))

    @pl.when(y == 0)
    def _():
        for n in range(4):
            here(n).start()

    @pl.when(y != 0)
    def _():
        for n in range(4):
            there(n).start()

    queries = []

    def ask(axis, n):
        d, other = PARTNERS[n]
        slot = axis * 8 + n
        copy = remote(
            q_ref.at[pl.ds(axis * BLK, BLK), pl.ds(pl.multiple_of(served(d, other) * G, G), G)], qs.at[slot],
            q_send.at[slot], q_recv.at[slot], partner(axis, d, other),
        )
        copy.start()
        queries.append(copy)

    own_q = []
    for axis in range(2):
        copy = pltpu.make_async_copy(
            q_ref.at[pl.ds(axis * BLK, BLK), pl.ds(pl.multiple_of(served(0, 0) * G, G), G)],
            qs.at[axis * 8 + 7], q_send.at[axis * 8 + 7],
        )
        copy.start()
        own_q.append(copy)
    asks = [(axis, n) for n in range(7) for axis in range(2)]

    def batch(size):
        for _ in range(min(size, len(asks))):
            ask(*asks.pop(0))

    batch(BATCHES[0])
    own_kv.wait()
    for copy in entry:
        copy.wait_recv()
    sent += entry

    count = len(PARTNERS)

    def pass_on(stream, shard, low, length, device):
        nonlocal count
        which, base, _, _ = stream
        piece = kv.at[which, pl.ds(shard * SHARD + base + low, length)]
        copy = remote(piece, piece, kv_send.at[count], kv_recv.at[count], device)
        count += 1
        copy.start()
        sent.append(copy)
        return copy

    def at(stream, one, two):
        return place(two, one) if stream[3] else place(one, two)

    def to(stream, ring, d):
        return slant(d) if stream[3] == (ring == 1) else (place(d, 0), head)

    first = {}
    second = {}
    for s in STREAMS:
        for d in (1, -1):
            first[s, d] = pass_on(s, me, 0, s[2], to(s, 1, d))
    for s in STREAMS:
        for d in (1, -1):
            second[s, 0, d] = pass_on(s, me, 0, s[2], to(s, 2, d))
    batch(BATCHES[1])
    first_far = []
    for d in (1, -1):
        for s in STREAMS:
            half = s[2] // 2
            first[s, d].wait_recv()
            shard = at(s, -d, 0)
            low = 0 if d == 1 else half
            first_far.append(pass_on(s, shard, low, half, to(s, 1, d)))
            for e in (1, -1):
                second[s, -d, e] = pass_on(s, shard, 0, s[2], to(s, 2, e))
    second_far = []

    def relay(line):
        for s in STREAMS:
            half = s[2] // 2
            for e in (1, -1):
                second[s, line, e].wait_recv()
                low = 0 if e == 1 else half
                second_far.append(pass_on(s, at(s, line, -e), low, half, to(s, 2, e)))

    batch(BATCHES[2])
    relay(0)
    for copy in first_far:
        copy.wait_recv()
    for s in STREAMS:
        for e in (1, -1):
            second[s, 2, e] = pass_on(s, at(s, 2, 0), 0, s[2], to(s, 2, e))
    batch(BATCHES[3])
    relay(-1)
    batch(BATCHES[4])
    relay(1)
    batch(BATCHES[5])
    relay(2)
    batch(14)

    @pl.when(y == 0)
    def _():
        for n in range(4):
            here(n).wait()

    @pl.when(y != 0)
    def _():
        for n in range(4):
            there(n).wait()

    index = [pltpu.make_async_copy(src, dst, local.at[2 + n]) for n, (_, src, dst) in enumerate(tables)]
    for copy in index:
        copy.start()
    for copy in index + own_q:
        copy.wait()
    for copy in second_far:
        copy.wait_recv()

    def turn(i):
        n = lax.div(i, 2)
        axis = lax.rem(i, 2)
        back = jnp.where(n < 2, 2, jnp.where(n < 6, 3 - 2 * lax.rem(n, 2), 0))
        other = jnp.where((n == 1) | ((n >= 4) & (n <= 6)), 1, 0)
        ctx = place(0, jnp.where(axis == 1, back, 0))
        return axis * 8 + n, axis, ctx, seat(jnp.where(axis == 0, back, 0), other)

    def fetch(i, side):
        _, axis, ctx, at_head = turn(i)
        b = ctx * SHARD + at_head * 2 + axis
        slash_live = sc_ref[0, b]
        vertical_live = vc_ref[0, b]
        for j in range(SLOTS):
            if j < NS:
                block = b - so_ref[j, 0, b]
                live = j < slash_live
            else:
                block = vb_ref[j - NS, 0, b]
                live = j - NS < vertical_live
            here = pl.ds(j * BLK, BLK)
            kg[side, here, :HD] = kv[0, block]
            bias = jnp.where(live, 0.0, NEG).astype(jnp.float32)
            kg[side, here, HD:] = jnp.full((BLK, HD), bias, jnp.float32).astype(jnp.bfloat16)
            vg[side, here, :HD] = kv[1, block]

    def arrive(i):
        @pl.when(i < SHARD - 2)
        def _():
            slot, _, ctx, at_head = turn(i)
            remote(qs.at[slot], qs.at[slot], q_send.at[slot], q_recv.at[slot], (ctx, at_head)).wait_recv()

    tokens = ROWS // G

    def score(i, half, side):
        rows = qs[turn(i)[0], pl.ds(half * tokens, tokens)].reshape(ROWS, HD)
        pick = (lax.broadcasted_iota(jnp.int32, (ROWS, HD), 1) == 0).astype(jnp.bfloat16)
        lhs = jnp.concatenate([rows, pick], axis=1)
        got = lax.dot_general(
            lhs, kg[side], (((1,), (1,)), ((), ())), preferred_element_type=jnp.float32
        )
        row = lax.broadcasted_iota(jnp.int32, (ROWS, 2 * BLK), 0) // G + half * tokens
        col = lax.broadcasted_iota(jnp.int32, (ROWS, 2 * BLK), 1)
        edge = jnp.where((col >= BLK) | (col <= row), got[:, : 2 * BLK], NEG)
        scores[half, :, : 2 * BLK] = edge
        scores[half, :, 2 * BLK :] = got[:, 2 * BLK :]
        top = jnp.maximum(
            jnp.max(edge, axis=1, keepdims=True), jnp.max(got[:, 2 * BLK :], axis=1, keepdims=True)
        )
        tops[half] = jnp.broadcast_to(top * FACTOR, (ROWS, HD))

    def answer(i, half, side):
        top = jnp.concatenate([tops[half]] * (KEYS // HD), axis=1)
        probs = jnp.exp2(scores[half] * FACTOR - top).astype(jnp.bfloat16)
        got = jnp.dot(probs, vg[side], preferred_element_type=jnp.float32)
        out = (got[:, :HD] / got[:, HD:]).astype(jnp.bfloat16)
        os[turn(i)[0], pl.ds(half * tokens, tokens)] = out.reshape(tokens, G, HD)

    columns = pl.ds(pl.multiple_of(served(0, 0) * G, G), G)

    def give(i):
        slot, axis, ctx, at_head = turn(i)
        rows = pl.ds(axis * BLK, BLK)
        return remote(
            os.at[slot], o_ref.at[rows, columns], o_send.at[slot], o_recv.at[slot], (ctx, at_head)
        )

    def keep(part):
        return pltpu.make_async_copy(
            os.at[part * 8 + 7], o_ref.at[pl.ds(part * BLK, BLK), columns], o_send.at[part * 8 + 7]
        )

    vg[:, :, HD:] = jnp.ones((2, KEYS, HD), jnp.bfloat16)
    fetch(0, 0)
    arrive(0)
    score(0, 0, 0)

    def step(i, carry):
        side = lax.rem(i, 2)
        later = jnp.minimum(i + 1, SHARD - 1)

        @pl.when((i >= 1) & (i <= SHARD - 2))
        def _():
            give(i - 1).start()

        arrive(i + 1)
        score(i, 1, side)
        answer(i, 0, side)
        fetch(later, 1 - side)
        score(later, 0, 1 - side)
        answer(i, 1, side)
        return carry

    lax.fori_loop(0, SHARD, step, 0)
    for part in range(2):
        keep(part).start()
    for copy in sent + queries:
        copy.wait_send()
    for part in range(2):
        keep(part).wait()

    def finish(i, carry):
        give(i).wait()
        return carry

    lax.fori_loop(0, SHARD - 2, finish, 0)


def on_device(query_states, key_states, value_states, so, sc, vb, vc):
    hbm = pl.BlockSpec(memory_space=pl.ANY)
    vmem = pl.BlockSpec(memory_space=pltpu.VMEM)
    bf16 = jnp.bfloat16
    so, vb = jnp.transpose(so, (2, 0, 1)), jnp.transpose(vb, (2, 0, 1))
    return pl.pallas_call(
        kernel,
        out_shape=pltpu.VMEM(query_states.shape, query_states.dtype),
        in_specs=[hbm] * 7,
        out_specs=vmem,
        scratch_shapes=[
            pltpu.SMEM(so.shape, jnp.int32),
            pltpu.SMEM(sc.shape, jnp.int32),
            pltpu.SMEM(vb.shape, jnp.int32),
            pltpu.SMEM(vc.shape, jnp.int32),
            pltpu.VMEM(so.shape, jnp.int32),
            pltpu.VMEM(sc.shape, jnp.int32),
            pltpu.VMEM(vb.shape, jnp.int32),
            pltpu.VMEM(vc.shape, jnp.int32),
            pltpu.VMEM(key_states.shape, bf16),
            pltpu.VMEM(value_states.shape, bf16),
            pltpu.VMEM((HEADS, 2, 2, BLK, HD), bf16),
            pltpu.VMEM((SHARD, BLK, G, HD), bf16),
            pltpu.VMEM((2, BLOCKS, BLK, HD), bf16),
            pltpu.VMEM((SHARD, BLK, G, HD), bf16),
            pltpu.VMEM((2, KEYS, 2 * HD), bf16),
            pltpu.VMEM((2, KEYS, 2 * HD), bf16),
            pltpu.VMEM((2, ROWS, KEYS), jnp.float32),
            pltpu.VMEM((2, ROWS, HD), jnp.float32),
            pltpu.SemaphoreType.DMA((SHARD,)),
            pltpu.SemaphoreType.DMA((SHARD,)),
            pltpu.SemaphoreType.DMA((8 + 20 * len(STREAMS),)),
            pltpu.SemaphoreType.DMA((8 + 20 * len(STREAMS),)),
            pltpu.SemaphoreType.DMA((SHARD,)),
            pltpu.SemaphoreType.DMA((SHARD,)),
            pltpu.SemaphoreType.DMA((6,)),
            pltpu.SemaphoreType.DMA((8,)),
            pltpu.SemaphoreType.DMA((4,)),
        ],
        compiler_params=pltpu.CompilerParams(
            collective_id=0, has_side_effects=True, vmem_limit_bytes=62_700_000
        ),
    )(so, sc, vb, vc, query_states, key_states, value_states)


def solution(mesh):
    token = P(("ctx", "head"), None, None)
    in_specs = (token,) * 3 + (P("head", None, None), P("head", None)) * 2
    return jax.shard_map(
        on_device, mesh=mesh, in_specs=in_specs, out_specs=token, check_vma=False
    )
```

```python
import math

import jax
import jax.numpy as jnp
from jax import lax
from jax.experimental import pallas as pl
from jax.experimental.pallas import tpu as pltpu
from jax.sharding import PartitionSpec as P

BLK = 64
G = 16
NS = 12
NV = 12
HD = 128
SLOTS = NS + NV
KEYS = SLOTS * BLK
ROWS = 512
RING = 4
HEADS = 2 * RING
SHARD = 2 * HEADS
BLOCKS = RING * RING * SHARD
NEG = -1e30
FACTOR = HD ** -0.5 * math.log2(math.e)
MESH = pl.DeviceIdType.MESH
PARTNERS = ((2, 0), (2, 1), (1, 0), (3, 0), (1, 1), (3, 1), (0, 1), (0, 0))

STREAMS = ((0, 0, 16, True), (1, 0, 8, True), (1, 8, 8, False))
BATCHES = (0, 0, 2, 4, 4, 4)


def remote(src, dst, send, recv, device):
    return pltpu.make_async_remote_copy(
        src_ref=src, dst_ref=dst, send_sem=send, recv_sem=recv, device_id=device, device_id_type=MESH
    )


def kernel(
    so_hbm, sc_hbm, vb_hbm, vc_hbm, q_ref, k_hbm, v_hbm, o_ref,
    so_ref, sc_ref, vb_ref, vc_ref, so_in, sc_in, vb_in, vc_in, k_ref, v_ref, kv_ref, qs, kv, os, kg, vg, scores, tops,
    q_send, q_recv, kv_send, kv_recv, o_send, o_recv, local, t_send, t_recv,
):
    me, head = lax.axis_index("ctx"), lax.axis_index("head")
    z, y = lax.div(me, RING), lax.rem(me, RING)
    x, core = lax.div(head, 2), lax.rem(head, 2)

    def wrap(a):
        return lax.rem(a + RING, RING)

    def place(dz, dy):
        return wrap(z + dz) * RING + wrap(y + dy)

    def seat(dx, other):
        return wrap(x + dx) * 2 + lax.rem(core + other, 2)

    def served(d, other):
        return lax.rem(x + y + d + RING, RING) * 2 + lax.rem(core + other, 2)

    def partner(axis, d, other):
        return (me, seat(d, other)) if axis == 0 else (place(0, d), seat(0, other))

    def slant(d):
        return place(0, d), seat(-d, 0)

    loads = [
        pltpu.make_async_copy(src, dst, local.at[n])
        for n, (src, dst) in enumerate(((k_hbm, k_ref), (v_hbm, v_ref)))
    ]
    for copy in loads:
        copy.start()

    peers = [partner(0, d, other) for d, other in PARTNERS[:-1]]
    peers += [partner(1, d, other) for d, other in PARTNERS[:-2]]
    peers += [slant(1), slant(-1), (place(1, 0), head), (place(-1, 0), head)]
    barrier = pltpu.get_barrier_semaphore()
    for peer in peers:
        pl.semaphore_signal(barrier, inc=1, device_id=peer, device_id_type=MESH)
    for copy in loads:
        copy.wait()
    for which, ref in ((0, k_ref), (1, v_ref)):
        for n in range(HEADS):
            kv_ref[n, which] = ref[:, n, :].reshape(2, BLK, HD)
    pl.semaphore_wait(barrier, len(peers))

    mine = pl.ds(me * SHARD + head * 2, 2)
    sent = []
    entry = []
    for n, (d, other) in enumerate(PARTNERS[:-1]):
        copy = remote(
            kv_ref.at[served(d, other)], kv.at[:, mine], kv_send.at[n], kv_recv.at[n], partner(0, d, other)
        )
        copy.start()
        entry.append(copy)
    own_kv = pltpu.make_async_copy(kv_ref.at[served(0, 0)], kv.at[:, mine], kv_send.at[7])
    own_kv.start()
    tables = ((so_hbm, so_in, so_ref), (sc_hbm, sc_in, sc_ref), (vb_hbm, vb_in, vb_ref), (vc_hbm, vc_in, vc_ref))

    def here(n):
        return pltpu.make_async_copy(tables[n][0], tables[n][1], t_send.at[n])

    def there(n):
        return remote(tables[n][0], tables[n][1], t_send.at[4 + n], t_recv.at[n], (me, seat(-y, 0)))

    @pl.when(y == 0)
    def _():
        for n in range(4):
            here(n).start()

    @pl.when(y != 0)
    def _():
        for n in range(4):
            there(n).start()

    queries = []

    def ask(axis, n):
        d, other = PARTNERS[n]
        slot = axis * 8 + n
        copy = remote(
            q_ref.at[pl.ds(axis * BLK, BLK), pl.ds(pl.multiple_of(served(d, other) * G, G), G)], qs.at[slot],
            q_send.at[slot], q_recv.at[slot], partner(axis, d, other),
        )
        copy.start()
        queries.append(copy)

    own_q = []
    for axis in range(2):
        copy = pltpu.make_async_copy(
            q_ref.at[pl.ds(axis * BLK, BLK), pl.ds(pl.multiple_of(served(0, 0) * G, G), G)],
            qs.at[axis * 8 + 7], q_send.at[axis * 8 + 7],
        )
        copy.start()
        own_q.append(copy)
    asks = [(axis, n) for n in range(7) for axis in range(2)]

    def batch(size):
        for _ in range(min(size, len(asks))):
            ask(*asks.pop(0))

    batch(BATCHES[0])
    own_kv.wait()
    for copy in entry:
        copy.wait_recv()
    sent += entry

    count = len(PARTNERS)

    def pass_on(stream, shard, low, length, device):
        nonlocal count
        which, base, _, _ = stream
        piece = kv.at[which, pl.ds(shard * SHARD + base + low, length)]
        copy = remote(piece, piece, kv_send.at[count], kv_recv.at[count], device)
        count += 1
        copy.start()
        sent.append(copy)
        return copy

    def at(stream, one, two):
        return place(two, one) if stream[3] else place(one, two)

    def to(stream, ring, d):
        return slant(d) if stream[3] == (ring == 1) else (place(d, 0), head)

    first = {}
    second = {}
    for s in STREAMS:
        for d in (1, -1):
            first[s, d] = pass_on(s, me, 0, s[2], to(s, 1, d))
    for s in STREAMS:
        for d in (1, -1):
            second[s, 0, d] = pass_on(s, me, 0, s[2], to(s, 2, d))
    @pl.when(y == 0)
    def _():
        for n in range(4):
            here(n).wait()

    @pl.when(y != 0)
    def _():
        for n in range(4):
            there(n).wait()

    index = [pltpu.make_async_copy(src, dst, local.at[2 + n]) for n, (_, src, dst) in enumerate(tables)]
    for copy in index:
        copy.start()
    batch(BATCHES[1])
    first_far = []
    for d in (1, -1):
        for s in STREAMS:
            half = s[2] // 2
            first[s, d].wait_recv()
            shard = at(s, -d, 0)
            low = 0 if d == 1 else half
            first_far.append(pass_on(s, shard, low, half, to(s, 1, d)))
            for e in (1, -1):
                second[s, -d, e] = pass_on(s, shard, 0, s[2], to(s, 2, e))
    second_far = []

    def relay(line):
        for s in STREAMS:
            half = s[2] // 2
            for e in (1, -1):
                second[s, line, e].wait_recv()
                low = 0 if e == 1 else half
                second_far.append(pass_on(s, at(s, line, -e), low, half, to(s, 2, e)))

    batch(BATCHES[2])
    relay(0)
    for copy in first_far:
        copy.wait_recv()
    for s in STREAMS:
        for e in (1, -1):
            second[s, 2, e] = pass_on(s, at(s, 2, 0), 0, s[2], to(s, 2, e))
    batch(BATCHES[3])
    relay(-1)
    batch(BATCHES[4])
    relay(1)
    batch(BATCHES[5])
    relay(2)
    batch(14)

    for copy in index + own_q:
        copy.wait()
    for copy in second_far:
        copy.wait_recv()

    def turn(i):
        n = lax.div(i, 2)
        axis = lax.rem(i, 2)
        back = jnp.where(n < 2, 2, jnp.where(n < 6, 3 - 2 * lax.rem(n, 2), 0))
        other = jnp.where((n == 1) | ((n >= 4) & (n <= 6)), 1, 0)
        ctx = place(0, jnp.where(axis == 1, back, 0))
        return axis * 8 + n, axis, ctx, seat(jnp.where(axis == 0, back, 0), other)

    def fetch(i, side):
        _, axis, ctx, at_head = turn(i)
        b = ctx * SHARD + at_head * 2 + axis
        slash_live = sc_ref[0, b]
        vertical_live = vc_ref[0, b]
        for j in range(SLOTS):
            if j < NS:
                block = b - so_ref[j, 0, b]
                live = j < slash_live
            else:
                block = vb_ref[j - NS, 0, b]
                live = j - NS < vertical_live
            here = pl.ds(j * BLK, BLK)
            kg[side, here, :HD] = kv[0, block]
            bias = jnp.where(live, 0.0, NEG).astype(jnp.float32)
            kg[side, here, HD:] = jnp.full((BLK, HD), bias, jnp.float32).astype(jnp.bfloat16)
            vg[side, here, :HD] = kv[1, block]

    def arrive(i):
        @pl.when(i < SHARD - 2)
        def _():
            slot, _, ctx, at_head = turn(i)
            remote(qs.at[slot], qs.at[slot], q_send.at[slot], q_recv.at[slot], (ctx, at_head)).wait_recv()

    tokens = ROWS // G

    def score(i, half, side):
        rows = qs[turn(i)[0], pl.ds(half * tokens, tokens)].reshape(ROWS, HD)
        pick = (lax.broadcasted_iota(jnp.int32, (ROWS, HD), 1) == 0).astype(jnp.bfloat16)
        lhs = jnp.concatenate([rows, pick], axis=1)
        got = lax.dot_general(
            lhs, kg[side], (((1,), (1,)), ((), ())), preferred_element_type=jnp.float32
        )
        row = lax.broadcasted_iota(jnp.int32, (ROWS, 2 * BLK), 0) // G + half * tokens
        col = lax.broadcasted_iota(jnp.int32, (ROWS, 2 * BLK), 1)
        edge = jnp.where((col >= BLK) | (col <= row), got[:, : 2 * BLK], NEG)
        scores[half, :, : 2 * BLK] = edge
        scores[half, :, 2 * BLK :] = got[:, 2 * BLK :]
        top = jnp.maximum(
            jnp.max(edge, axis=1, keepdims=True), jnp.max(got[:, 2 * BLK :], axis=1, keepdims=True)
        )
        tops[half] = jnp.broadcast_to(top * FACTOR, (ROWS, HD))

    def answer(i, half, side):
        top = jnp.concatenate([tops[half]] * (KEYS // HD), axis=1)
        probs = jnp.exp2(scores[half] * FACTOR - top).astype(jnp.bfloat16)
        got = jnp.dot(probs, vg[side], preferred_element_type=jnp.float32)
        out = (got[:, :HD] / got[:, HD:]).astype(jnp.bfloat16)
        os[turn(i)[0], pl.ds(half * tokens, tokens)] = out.reshape(tokens, G, HD)

    columns = pl.ds(pl.multiple_of(served(0, 0) * G, G), G)

    def give(i):
        slot, axis, ctx, at_head = turn(i)
        rows = pl.ds(axis * BLK, BLK)
        return remote(
            os.at[slot], o_ref.at[rows, columns], o_send.at[slot], o_recv.at[slot], (ctx, at_head)
        )

    def keep(part):
        return pltpu.make_async_copy(
            os.at[part * 8 + 7], o_ref.at[pl.ds(part * BLK, BLK), columns], o_send.at[part * 8 + 7]
        )

    vg[:, :, HD:] = jnp.ones((2, KEYS, HD), jnp.bfloat16)
    fetch(0, 0)
    arrive(0)
    score(0, 0, 0)

    def step(i, carry):
        side = lax.rem(i, 2)
        later = jnp.minimum(i + 1, SHARD - 1)

        @pl.when((i >= 1) & (i <= SHARD - 2))
        def _():
            give(i - 1).start()

        arrive(i + 1)
        score(i, 1, side)
        answer(i, 0, side)
        fetch(later, 1 - side)
        score(later, 0, 1 - side)
        answer(i, 1, side)
        return carry

    lax.fori_loop(0, SHARD, step, 0)
    for part in range(2):
        keep(part).start()
    for copy in sent + queries:
        copy.wait_send()
    for part in range(2):
        keep(part).wait()

    def finish(i, carry):
        give(i).wait()
        return carry

    lax.fori_loop(0, SHARD - 2, finish, 0)


def on_device(query_states, key_states, value_states, so, sc, vb, vc):
    hbm = pl.BlockSpec(memory_space=pl.ANY)
    vmem = pl.BlockSpec(memory_space=pltpu.VMEM)
    bf16 = jnp.bfloat16
    so, vb = jnp.transpose(so, (2, 0, 1)), jnp.transpose(vb, (2, 0, 1))
    return pl.pallas_call(
        kernel,
        out_shape=pltpu.VMEM(query_states.shape, query_states.dtype),
        in_specs=[hbm] * 7,
        out_specs=vmem,
        scratch_shapes=[
            pltpu.SMEM(so.shape, jnp.int32),
            pltpu.SMEM(sc.shape, jnp.int32),
            pltpu.SMEM(vb.shape, jnp.int32),
            pltpu.SMEM(vc.shape, jnp.int32),
            pltpu.VMEM(so.shape, jnp.int32),
            pltpu.VMEM(sc.shape, jnp.int32),
            pltpu.VMEM(vb.shape, jnp.int32),
            pltpu.VMEM(vc.shape, jnp.int32),
            pltpu.VMEM(key_states.shape, bf16),
            pltpu.VMEM(value_states.shape, bf16),
            pltpu.VMEM((HEADS, 2, 2, BLK, HD), bf16),
            pltpu.VMEM((SHARD, BLK, G, HD), bf16),
            pltpu.VMEM((2, BLOCKS, BLK, HD), bf16),
            pltpu.VMEM((SHARD, BLK, G, HD), bf16),
            pltpu.VMEM((2, KEYS, 2 * HD), bf16),
            pltpu.VMEM((2, KEYS, 2 * HD), bf16),
            pltpu.VMEM((2, ROWS, KEYS), jnp.float32),
            pltpu.VMEM((2, ROWS, HD), jnp.float32),
            pltpu.SemaphoreType.DMA((SHARD,)),
            pltpu.SemaphoreType.DMA((SHARD,)),
            pltpu.SemaphoreType.DMA((8 + 20 * len(STREAMS),)),
            pltpu.SemaphoreType.DMA((8 + 20 * len(STREAMS),)),
            pltpu.SemaphoreType.DMA((SHARD,)),
            pltpu.SemaphoreType.DMA((SHARD,)),
            pltpu.SemaphoreType.DMA((6,)),
            pltpu.SemaphoreType.DMA((8,)),
            pltpu.SemaphoreType.DMA((4,)),
        ],
        compiler_params=pltpu.CompilerParams(
            collective_id=0, has_side_effects=True, vmem_limit_bytes=62_700_000
        ),
    )(so, sc, vb, vc, query_states, key_states, value_states)


def solution(mesh):
    token = P(("ctx", "head"), None, None)
    in_specs = (token,) * 3 + (P("head", None, None), P("head", None)) * 2
    return jax.shard_map(
        on_device, mesh=mesh, in_specs=in_specs, out_specs=token, check_vma=False
    )
```

```python
import math

import jax
import jax.numpy as jnp
from jax import lax
from jax.experimental import pallas as pl
from jax.experimental.pallas import tpu as pltpu
from jax.sharding import PartitionSpec as P

BLK = 64
G = 16
NS = 12
NV = 12
HD = 128
SLOTS = NS + NV
KEYS = SLOTS * BLK
ROWS = 512
RING = 4
HEADS = 2 * RING
SHARD = 2 * HEADS
BLOCKS = RING * RING * SHARD
NEG = -1e30
FACTOR = HD ** -0.5 * math.log2(math.e)
MESH = pl.DeviceIdType.MESH
PARTNERS = ((2, 0), (2, 1), (1, 0), (3, 0), (1, 1), (3, 1), (0, 1), (0, 0))

STREAMS = ((0, 0, 16, True), (1, 0, 8, True), (1, 8, 8, False))
BATCHES = (0, 0, 2, 4, 4, 4)


def remote(src, dst, send, recv, device):
    return pltpu.make_async_remote_copy(
        src_ref=src, dst_ref=dst, send_sem=send, recv_sem=recv, device_id=device, device_id_type=MESH
    )


def kernel(
    so_hbm, sc_hbm, vb_hbm, vc_hbm, q_ref, k_hbm, v_hbm, o_ref,
    so_ref, sc_ref, vb_ref, vc_ref, so_in, sc_in, vb_in, vc_in, k_ref, v_ref, kv_ref, qs, kv, os, kg, vg, scores, tops,
    q_send, q_recv, kv_send, kv_recv, o_send, o_recv, local, t_send, t_recv,
):
    me, head = lax.axis_index("ctx"), lax.axis_index("head")
    z, y = lax.div(me, RING), lax.rem(me, RING)
    x, core = lax.div(head, 2), lax.rem(head, 2)

    def wrap(a):
        return lax.rem(a + RING, RING)

    def place(dz, dy):
        return wrap(z + dz) * RING + wrap(y + dy)

    def seat(dx, other):
        return wrap(x + dx) * 2 + lax.rem(core + other, 2)

    def served(d, other):
        return lax.rem(x + y + d + RING, RING) * 2 + lax.rem(core + other, 2)

    def partner(axis, d, other):
        return (me, seat(d, other)) if axis == 0 else (place(0, d), seat(0, other))

    def slant(d):
        return place(0, d), seat(-d, 0)

    loads = [
        pltpu.make_async_copy(src, dst, local.at[n])
        for n, (src, dst) in enumerate(((k_hbm, k_ref), (v_hbm, v_ref)))
    ]
    for copy in loads:
        copy.start()

    peers = [partner(0, d, other) for d, other in PARTNERS[:-1]]
    peers += [partner(1, d, other) for d, other in PARTNERS[:-2]]
    peers += [slant(1), slant(-1), (place(1, 0), head), (place(-1, 0), head)]
    barrier = pltpu.get_barrier_semaphore()
    for peer in peers:
        pl.semaphore_signal(barrier, inc=1, device_id=peer, device_id_type=MESH)
    for copy in loads:
        copy.wait()
    for which, ref in ((0, k_ref), (1, v_ref)):
        for n in range(HEADS):
            kv_ref[n, which] = ref[:, n, :].reshape(2, BLK, HD)
    vg[:, :, HD:] = jnp.ones((2, KEYS, HD), jnp.bfloat16)
    pl.semaphore_wait(barrier, len(peers))

    mine = pl.ds(me * SHARD + head * 2, 2)
    sent = []
    entry = []
    for n, (d, other) in enumerate(PARTNERS[:-1]):
        copy = remote(
            kv_ref.at[served(d, other)], kv.at[:, mine], kv_send.at[n], kv_recv.at[n], partner(0, d, other)
        )
        copy.start()
        entry.append(copy)
    own_kv = pltpu.make_async_copy(kv_ref.at[served(0, 0)], kv.at[:, mine], kv_send.at[7])
    own_kv.start()
    tables = ((so_hbm, so_in, so_ref), (sc_hbm, sc_in, sc_ref), (vb_hbm, vb_in, vb_ref), (vc_hbm, vc_in, vc_ref))

    def here(n):
        return pltpu.make_async_copy(tables[n][0], tables[n][1], t_send.at[n])

    def there(n):
        return remote(tables[n][0], tables[n][1], t_send.at[4 + n], t_recv.at[n], (me, seat(-y, 0)))

    @pl.when(y == 0)
    def _():
        for n in range(4):
            here(n).start()

    @pl.when(y != 0)
    def _():
        for n in range(4):
            there(n).start()

    queries = []

    def ask(axis, n):
        d, other = PARTNERS[n]
        slot = axis * 8 + n
        copy = remote(
            q_ref.at[pl.ds(axis * BLK, BLK), pl.ds(pl.multiple_of(served(d, other) * G, G), G)], qs.at[slot],
            q_send.at[slot], q_recv.at[slot], partner(axis, d, other),
        )
        copy.start()
        queries.append(copy)

    own_q = []
    for axis in range(2):
        copy = pltpu.make_async_copy(
            q_ref.at[pl.ds(axis * BLK, BLK), pl.ds(pl.multiple_of(served(0, 0) * G, G), G)],
            qs.at[axis * 8 + 7], q_send.at[axis * 8 + 7],
        )
        copy.start()
        own_q.append(copy)
    asks = [(axis, n) for n in range(7) for axis in range(2)]

    def batch(size):
        for _ in range(min(size, len(asks))):
            ask(*asks.pop(0))

    batch(BATCHES[0])
    own_kv.wait()
    for copy in entry:
        copy.wait_recv()
    sent += entry

    count = len(PARTNERS)

    def pass_on(stream, shard, low, length, device):
        nonlocal count
        which, base, _, _ = stream
        piece = kv.at[which, pl.ds(shard * SHARD + base + low, length)]
        copy = remote(piece, piece, kv_send.at[count], kv_recv.at[count], device)
        count += 1
        copy.start()
        sent.append(copy)
        return copy

    def at(stream, one, two):
        return place(two, one) if stream[3] else place(one, two)

    def to(stream, ring, d):
        return slant(d) if stream[3] == (ring == 1) else (place(d, 0), head)

    first = {}
    second = {}
    for s in STREAMS:
        for d in (1, -1):
            first[s, d] = pass_on(s, me, 0, s[2], to(s, 1, d))
    for s in STREAMS:
        for d in (1, -1):
            second[s, 0, d] = pass_on(s, me, 0, s[2], to(s, 2, d))
    @pl.when(y == 0)
    def _():
        for n in range(4):
            here(n).wait()

    @pl.when(y != 0)
    def _():
        for n in range(4):
            there(n).wait()

    index = [pltpu.make_async_copy(src, dst, local.at[2 + n]) for n, (_, src, dst) in enumerate(tables)]
    for copy in index:
        copy.start()
    batch(BATCHES[1])
    first_far = []
    for d in (1, -1):
        for s in STREAMS:
            half = s[2] // 2
            first[s, d].wait_recv()
            shard = at(s, -d, 0)
            low = 0 if d == 1 else half
            first_far.append(pass_on(s, shard, low, half, to(s, 1, d)))
            for e in (1, -1):
                second[s, -d, e] = pass_on(s, shard, 0, s[2], to(s, 2, e))
    second_far = []

    def relay(line):
        for s in STREAMS:
            half = s[2] // 2
            for e in (1, -1):
                second[s, line, e].wait_recv()
                low = 0 if e == 1 else half
                second_far.append(pass_on(s, at(s, line, -e), low, half, to(s, 2, e)))

    batch(BATCHES[2])
    relay(0)
    for copy in first_far:
        copy.wait_recv()
    for s in STREAMS:
        for e in (1, -1):
            second[s, 2, e] = pass_on(s, at(s, 2, 0), 0, s[2], to(s, 2, e))
    batch(BATCHES[3])
    relay(-1)
    batch(BATCHES[4])
    relay(1)
    batch(BATCHES[5])
    relay(2)
    batch(14)

    for copy in index + own_q:
        copy.wait()
    for copy in second_far:
        copy.wait_recv()

    def turn(i):
        n = lax.div(i, 2)
        axis = lax.rem(i, 2)
        back = jnp.where(n < 2, 2, jnp.where(n < 6, 3 - 2 * lax.rem(n, 2), 0))
        other = jnp.where((n == 1) | ((n >= 4) & (n <= 6)), 1, 0)
        ctx = place(0, jnp.where(axis == 1, back, 0))
        return axis * 8 + n, axis, ctx, seat(jnp.where(axis == 0, back, 0), other)

    def fetch(i, side):
        _, axis, ctx, at_head = turn(i)
        b = ctx * SHARD + at_head * 2 + axis
        slash_live = sc_ref[0, b]
        vertical_live = vc_ref[0, b]
        for j in range(SLOTS):
            if j < NS:
                block = b - so_ref[j, 0, b]
                live = j < slash_live
            else:
                block = vb_ref[j - NS, 0, b]
                live = j - NS < vertical_live
            here = pl.ds(j * BLK, BLK)
            kg[side, here, :HD] = kv[0, block]
            bias = jnp.where(live, 0.0, NEG).astype(jnp.float32)
            kg[side, here, HD:] = jnp.full((BLK, HD), bias, jnp.float32).astype(jnp.bfloat16)
            vg[side, here, :HD] = kv[1, block]

    def arrive(i):
        @pl.when(i < SHARD - 2)
        def _():
            slot, _, ctx, at_head = turn(i)
            remote(qs.at[slot], qs.at[slot], q_send.at[slot], q_recv.at[slot], (ctx, at_head)).wait_recv()

    tokens = ROWS // G

    def score(i, half, side):
        rows = qs[turn(i)[0], pl.ds(half * tokens, tokens)].reshape(ROWS, HD)
        pick = (lax.broadcasted_iota(jnp.int32, (ROWS, HD), 1) == 0).astype(jnp.bfloat16)
        lhs = jnp.concatenate([rows, pick], axis=1)
        got = lax.dot_general(
            lhs, kg[side], (((1,), (1,)), ((), ())), preferred_element_type=jnp.float32
        )
        row = lax.broadcasted_iota(jnp.int32, (ROWS, 2 * BLK), 0) // G + half * tokens
        col = lax.broadcasted_iota(jnp.int32, (ROWS, 2 * BLK), 1)
        edge = jnp.where((col >= BLK) | (col <= row), got[:, : 2 * BLK], NEG)
        scores[half, :, : 2 * BLK] = edge
        scores[half, :, 2 * BLK :] = got[:, 2 * BLK :]
        top = jnp.maximum(
            jnp.max(edge, axis=1, keepdims=True), jnp.max(got[:, 2 * BLK :], axis=1, keepdims=True)
        )
        tops[half] = jnp.broadcast_to(top * FACTOR, (ROWS, HD))

    def answer(i, half, side):
        top = jnp.concatenate([tops[half]] * (KEYS // HD), axis=1)
        probs = jnp.exp2(scores[half] * FACTOR - top).astype(jnp.bfloat16)
        got = jnp.dot(probs, vg[side], preferred_element_type=jnp.float32)
        out = (got[:, :HD] / got[:, HD:]).astype(jnp.bfloat16)
        os[turn(i)[0], pl.ds(half * tokens, tokens)] = out.reshape(tokens, G, HD)

    columns = pl.ds(pl.multiple_of(served(0, 0) * G, G), G)

    def give(i):
        slot, axis, ctx, at_head = turn(i)
        rows = pl.ds(axis * BLK, BLK)
        return remote(
            os.at[slot], o_ref.at[rows, columns], o_send.at[slot], o_recv.at[slot], (ctx, at_head)
        )

    def keep(part):
        return pltpu.make_async_copy(
            os.at[part * 8 + 7], o_ref.at[pl.ds(part * BLK, BLK), columns], o_send.at[part * 8 + 7]
        )

    fetch(0, 0)
    arrive(0)
    score(0, 0, 0)

    def step(i, carry):
        side = lax.rem(i, 2)
        later = jnp.minimum(i + 1, SHARD - 1)

        @pl.when((i >= 1) & (i <= SHARD - 2))
        def _():
            give(i - 1).start()

        arrive(i + 1)
        score(i, 1, side)
        answer(i, 0, side)
        fetch(later, 1 - side)
        score(later, 0, 1 - side)
        answer(i, 1, side)
        return carry

    lax.fori_loop(0, SHARD, step, 0)
    for part in range(2):
        keep(part).start()
    for copy in sent + queries:
        copy.wait_send()
    for part in range(2):
        keep(part).wait()

    def finish(i, carry):
        give(i).wait()
        return carry

    lax.fori_loop(0, SHARD - 2, finish, 0)


def on_device(query_states, key_states, value_states, so, sc, vb, vc):
    hbm = pl.BlockSpec(memory_space=pl.ANY)
    vmem = pl.BlockSpec(memory_space=pltpu.VMEM)
    bf16 = jnp.bfloat16
    so, vb = jnp.transpose(so, (2, 0, 1)), jnp.transpose(vb, (2, 0, 1))
    return pl.pallas_call(
        kernel,
        out_shape=pltpu.VMEM(query_states.shape, query_states.dtype),
        in_specs=[hbm] * 7,
        out_specs=vmem,
        scratch_shapes=[
            pltpu.SMEM(so.shape, jnp.int32),
            pltpu.SMEM(sc.shape, jnp.int32),
            pltpu.SMEM(vb.shape, jnp.int32),
            pltpu.SMEM(vc.shape, jnp.int32),
            pltpu.VMEM(so.shape, jnp.int32),
            pltpu.VMEM(sc.shape, jnp.int32),
            pltpu.VMEM(vb.shape, jnp.int32),
            pltpu.VMEM(vc.shape, jnp.int32),
            pltpu.VMEM(key_states.shape, bf16),
            pltpu.VMEM(value_states.shape, bf16),
            pltpu.VMEM((HEADS, 2, 2, BLK, HD), bf16),
            pltpu.VMEM((SHARD, BLK, G, HD), bf16),
            pltpu.VMEM((2, BLOCKS, BLK, HD), bf16),
            pltpu.VMEM((SHARD, BLK, G, HD), bf16),
            pltpu.VMEM((2, KEYS, 2 * HD), bf16),
            pltpu.VMEM((2, KEYS, 2 * HD), bf16),
            pltpu.VMEM((2, ROWS, KEYS), jnp.float32),
            pltpu.VMEM((2, ROWS, HD), jnp.float32),
            pltpu.SemaphoreType.DMA((SHARD,)),
            pltpu.SemaphoreType.DMA((SHARD,)),
            pltpu.SemaphoreType.DMA((8 + 20 * len(STREAMS),)),
            pltpu.SemaphoreType.DMA((8 + 20 * len(STREAMS),)),
            pltpu.SemaphoreType.DMA((SHARD,)),
            pltpu.SemaphoreType.DMA((SHARD,)),
            pltpu.SemaphoreType.DMA((6,)),
            pltpu.SemaphoreType.DMA((8,)),
            pltpu.SemaphoreType.DMA((4,)),
        ],
        compiler_params=pltpu.CompilerParams(
            collective_id=0, has_side_effects=True, vmem_limit_bytes=62_700_000
        ),
    )(so, sc, vb, vc, query_states, key_states, value_states)


def solution(mesh):
    token = P(("ctx", "head"), None, None)
    in_specs = (token,) * 3 + (P("head", None, None), P("head", None)) * 2
    return jax.shard_map(
        on_device, mesh=mesh, in_specs=in_specs, out_specs=token, check_vma=False
    )
```
